32 devices in a mesh: dp: 8 (over y, x, core), ctx: 4 (over z).
Axes of the slice: x: 2, y: 2, z: 4, core: 2. Of those that a mesh axis runs over, the one named last changes fastest.
Arguments:
- layer_input: bfloat16 [8, 2048, 1536], P('dp', 'ctx'), may hold values from -60 to 60
- attn_gain: bfloat16 [1536], P('dp'), may hold values from 0.5 to 1.5
- w_qkv: bfloat16 [1536, 3072], P('dp'), may hold values from -1 to 1
- w_out: bfloat16 [1536, 1536], P('dp'), may hold values from -2.5 to 2.5
- mlp_gain: bfloat16 [1536], P('dp'), may hold values from 0.5 to 1.5
- w_gate_up: bfloat16 [1536, 8192], P('dp'), may hold values from -0.15625 to 0.15625
- w_down: bfloat16 [4096, 1536], P('dp'), may hold values from -0.09375 to 0.09375
- cotangent: bfloat16 [8, 2048, 1536], P('dp', 'ctx'), may hold values from -6 to 6
Outputs:
- layer_output: bfloat16 [8, 2048, 1536], P('dp', 'ctx')
- input_grad: float32 [8, 2048, 1536], P('dp', 'ctx')
- attn_gain_grad: float32 [1536], P('dp')
- w_qkv_grad: float32 [1536, 3072], P('dp')
- w_out_grad: float32 [1536, 1536], P('dp')
- mlp_gain_grad: float32 [1536], P('dp')
- w_gate_up_grad: float32 [1536, 8192], P('dp')
- w_down_grad: float32 [4096, 1536], P('dp')
The draws below stay inside these ranges and needn't reach their ends.
All inputs are finite; a program needn't handle non-finite values.
Results may differ from the reference program's by a relative error of at most 0.02.
Values may be sent and summed in bfloat16 or wider, within the bound.
No kernel may reach another device: no remote copies, remote signals or barrier semaphores. Data moves between devices by JAX's collectives and lax.ppermute only.
A program may use at most 256 MiB of HBM per device.

```python
import math
import jax
import jax.numpy as jnp
from jax import lax

D = 1536
H = 16
KVH = 8
HD = 96
FF = 4096
SEQ_LEN = 2048
SEQS = 8


def draw_layer_input(key, part):
    first, second = jax.random.split(key, 2)
    scales = jnp.exp(jax.random.uniform(second, (SEQS, SEQ_LEN, 1), jnp.float32) * math.log(10.0))
    base = jnp.clip(jax.random.normal(first, (SEQS, SEQ_LEN, D), jnp.float32), -6.0, 6.0)
    return (base * scales).astype(jnp.bfloat16)


def draw_w_qkv(key, part):
    columns = H * HD + 2 * KVH * HD
    base = jnp.clip(jax.random.normal(key, (D, columns), jnp.float32), -6.0, 6.0)
    return (base * (1.0 / math.sqrt(D))).astype(jnp.bfloat16)


def shard_levels(key, shape, cuts, least, top_value):
    def one(position, blocks):
        heights = jax.random.uniform(jax.random.fold_in(jax.random.fold_in(key, 6), position), (blocks,), jnp.float32, least / len(cuts), top_value / len(cuts))
        return jnp.repeat(jnp.exp(heights), shape[position] // blocks).reshape((-1,) + (1,) * (len(shape) - position - 1))

    loudness = one(*cuts[0])
    for cut in cuts[1:]:
        loudness = loudness * one(*cut)
    return loudness


def scatter_about(key, extent, scale, reach, cuts=(), kind=jnp.bfloat16):
    level = shard_levels(key, extent, cuts, -0.22, 0.18) if cuts else 1.0
    entries = jax.random.normal(key, extent, jnp.float32) * scale * level
    return jnp.minimum(jnp.maximum(entries, -reach), reach).astype(kind)


def setup_inputs(seed: int = 0) -> dict:
    key_of = jax.random.split(jax.random.key(seed), 9)
    layer_input = draw_layer_input(jax.random.fold_in(key_of[8], 71), 0)
    attn_gain = jnp.clip(1.0 + 0.1 * jax.random.normal(key_of[1], (D,), jnp.float32), 0.5, 1.5).astype(jnp.bfloat16)
    w_qkv = draw_w_qkv(jax.random.fold_in(key_of[8], 71), 0)
    w_out = scatter_about(key_of[3], (H * HD, D), (max(D // 256, 1)) ** -0.5, 2.5, ((0, 8),))
    mlp_gain = jnp.clip(1.0 + 0.1 * jax.random.normal(key_of[4], (D,), jnp.float32), 0.5, 1.5).astype(jnp.bfloat16)
    w_gate_up = scatter_about(key_of[5], (D, 2 * FF), D ** -0.5, 0.15625, ((0, 8),))
    w_down = scatter_about(key_of[6], (FF, D), FF ** -0.5, 0.09375, ((0, 8),))
    cotangent = scatter_about(key_of[7], (SEQS, SEQ_LEN, D), 1.0, 6.0, ((0, 8), (1, 4)))
    return {"layer_input": layer_input, "attn_gain": attn_gain, "w_qkv": w_qkv, "w_out": w_out, "mlp_gain": mlp_gain, "w_gate_up": w_gate_up, "w_down": w_down, "cotangent": cotangent}


@jax.custom_vjp
def low(v):
    return lax.optimization_barrier(v.astype(jnp.bfloat16)).astype(jnp.float32)

@jax.custom_vjp
def low_back(v):
    return v

def low_keep(v):
    return (low(v), None)

def low_pass(kept, grad):
    return (grad,)

def back_keep(v):
    return (v, None)

def back_low(kept, grad):
    return (low(grad),)
low.defvjp(low_keep, low_pass)
low_back.defvjp(back_keep, back_low)
EPS = 1e-05
BASE = 100000.0
HIGHEST = lax.Precision.HIGHEST

def normalize(values, gain):
    return values * lax.rsqrt(lax.optimization_barrier(jnp.mean(values * values, axis=-1, keepdims=True)) + EPS) * gain

def rotate(values, cosines, sines):
    half = values.shape[-1] // 2
    first = values[..., :half]
    second = values[..., half:]
    return jnp.concatenate([first * cosines - second * sines, second * cosines + first * sines], axis=-1)

def attend(queries, keys, values):
    length = queries.shape[0]
    group = H // KVH
    block = math.gcd(length, 512)
    scale = 1.0 / math.sqrt(HD)
    key_pos = jnp.arange(length, dtype=jnp.int32)

    def one_block(pair):
        rows, begin = pair
        heads = rows.reshape(block, KVH, group, HD)
        scores = low_back(jnp.einsum('bkgd,tkd->kgbt', heads, keys, precision=HIGHEST) * scale)
        query_pos = begin + jnp.arange(block, dtype=jnp.int32)
        scores = jnp.where(key_pos[None, :] <= query_pos[:, None], scores, -1e+30)
        probs = low(jax.nn.softmax(scores, axis=-1))
        mixed = jnp.einsum('kgbt,tkd->bkgd', probs, values, precision=HIGHEST)
        return mixed.reshape(block, H * HD)
    starts = jnp.arange(length // block, dtype=jnp.int32) * block
    blocks = queries.reshape(length // block, block, H, HD)
    mixed = lax.map(jax.checkpoint(one_block), (blocks, starts))
    return mixed.reshape(length, H * HD)

def layer_forward(inputs, attn_gain, w_qkv, w_out, mlp_gain, w_gate_up, w_down):
    length = inputs.shape[0]
    q_width = H * HD
    kv_width = KVH * HD
    normed_a = low(normalize(inputs, attn_gain))
    proj = low_back(jnp.dot(normed_a, w_qkv, precision=HIGHEST))
    freq = BASE ** (-(jnp.arange(HD // 2, dtype=jnp.float32) * 2.0 / HD))
    angle = jnp.arange(length, dtype=jnp.float32)[:, None] * freq[None, :]
    cosines = jnp.cos(angle)[:, None, :]
    sines = jnp.sin(angle)[:, None, :]
    q_rot = low(rotate(proj[:, :q_width].reshape(length, H, HD), cosines, sines))
    k_rot = low(rotate(proj[:, q_width:q_width + kv_width].reshape(length, KVH, HD), cosines, sines))
    v_low = low(proj[:, q_width + kv_width:].reshape(length, KVH, HD))
    attn = attend(q_rot, k_rot, v_low)
    attn_low = low(low_back(attn))
    resid = inputs + low_back(jnp.dot(attn_low, w_out, precision=HIGHEST))
    normed_m = low(normalize(resid, mlp_gain))
    gate_up = low_back(jnp.dot(normed_m, w_gate_up, precision=HIGHEST))
    gate = gate_up[:, :FF]
    upper = gate_up[:, FF:]
    act = low(jax.nn.silu(gate) * upper)
    return resid + low_back(jnp.dot(act, w_down, precision=HIGHEST))

def reference(layer_input, attn_gain, w_qkv, w_out, mlp_gain, w_gate_up, w_down, cotangent):
    weights = tuple((w.astype(jnp.float32) for w in (attn_gain, w_qkv, w_out, mlp_gain, w_gate_up, w_down)))

    def one_sequence(totals, pair):
        inputs, grad_out = pair
        result, pull = jax.vjp(layer_forward, inputs.astype(jnp.float32), *weights)
        grads = pull(grad_out.astype(jnp.float32))
        totals = tuple((t + g for t, g in zip(totals, grads[1:])))
        return (totals, (result.astype(jnp.bfloat16), grads[0]))
    start = tuple((jnp.zeros(w.shape, jnp.float32) for w in weights))
    totals, (result, input_grad) = lax.scan(one_sequence, start, (layer_input, cotangent))
    return (result, input_grad, totals[0], totals[1], totals[2], totals[3], totals[4], totals[5])
```

```python
import functools
import math

import jax
import jax.numpy as jnp
from jax import lax
from jax.experimental import pallas as pl
from jax.experimental.pallas import tpu as pltpu
from jax.sharding import PartitionSpec as P

H = 16
KVH = 8
HD = 96
FF = 4096
GROUP = H // KVH
HALF = HD // 2
Q_WIDTH = H * HD
KV_WIDTH = KVH * HD
SCALE = 1.0 / math.sqrt(HD)
LOG2_SCALE = math.log2(math.e) * SCALE


EPS = 1e-05
BASE = 100000.0
F32 = jnp.float32
BF16 = jnp.bfloat16


def dot(first, second, first_dim, second_dim):
    return lax.dot_general(
        first,
        second,
        (((first_dim,), (second_dim,)), ((), ())),
        preferred_element_type=F32,
    )


def visible(size):
    key = lax.broadcasted_iota(jnp.int32, (size, size), 0)
    query = lax.broadcasted_iota(jnp.int32, (size, size), 1)
    return key <= query


def forward_first(q_ref, k_ref, v_ref, top_ref, total_ref, mixed_ref):
    for head in range(GROUP):
        rows = pl.ds(head * HD, HD)
        scores = dot(k_ref[...], q_ref[rows, :], 0, 0)
        scores = jnp.where(visible(scores.shape[0]), scores, -1e30)
        top = jnp.max(scores, axis=0, keepdims=True)
        weights = jnp.exp2(scores * LOG2_SCALE - top * LOG2_SCALE)
        top_ref[0, head : head + 1, :] = top
        total_ref[0, head : head + 1, :] = jnp.sum(weights, axis=0, keepdims=True)
        mixed_ref[rows, :] = dot(v_ref[...], weights.astype(BF16), 1, 0)


def forward_more(flag, q_ref, k_ref, v_ref, top_in, total_in, mixed_in, top_ref, total_ref, mixed_ref):
    @pl.when(flag[0] == 1)
    def _():
        for head in range(GROUP):
            rows = pl.ds(head * HD, HD)
            scores = dot(k_ref[...], q_ref[rows, :], 0, 0)
            before = top_in[0, head : head + 1, :]
            top = jnp.maximum(jnp.max(scores, axis=0, keepdims=True), before)
            weights = jnp.exp2(scores * LOG2_SCALE - top * LOG2_SCALE)
            fading = jnp.exp2((before - top) * LOG2_SCALE)
            top_ref[0, head : head + 1, :] = top
            total_ref[0, head : head + 1, :] = (
                jnp.sum(weights, axis=0, keepdims=True)
                + total_in[0, head : head + 1, :] * fading
            )
            mixed_ref[rows, :] = (
                dot(v_ref[...], weights.astype(BF16), 1, 0) + mixed_in[rows, :] * fading
            )

    @pl.when(flag[0] != 1)
    def _():
        top_ref[...] = top_in[...]
        total_ref[...] = total_in[...]
        mixed_ref[...] = mixed_in[...]


def forward_last(
    flag, q_ref, k_ref, v_ref, top_in, total_in, mixed_in, log_ref, attn_ref, low_ref, top_s, total_s
):
    forward_more(
        flag, q_ref, k_ref, v_ref, top_in, total_in, mixed_in, top_s, total_s, attn_ref
    )
    for head in range(GROUP):
        rows = pl.ds(head * HD, HD)
        total = total_s[0, head : head + 1, :]
        attn = attn_ref[rows, :] * (1.0 / total)
        attn_ref[rows, :] = attn
        low_ref[rows, :] = attn.astype(BF16)
        log_ref[0, head : head + 1, :] = top_s[0, head : head + 1, :] * LOG2_SCALE + jnp.log2(total)


def block_specs(length):
    stat = pl.BlockSpec((1, GROUP, length), lambda g, *_: (g, 0, 0))
    wide = pl.BlockSpec((GROUP * HD, length), lambda g, *_: (g, 0))
    keys = pl.BlockSpec((HD, length), lambda g, *_: (g, 0))
    values = pl.BlockSpec((HD, length), lambda g, *_: (g + KVH, 0))
    return stat, wide, keys, values


def costs(length, products, arrays):
    return pl.CostEstimate(
        flops=2 * products * H * length * length * HD,
        bytes_accessed=arrays * Q_WIDTH * length,
        transcendentals=H * length * length,
    )


def attend_forward(queries, blocks, flags):
    length = queries.shape[1]
    stat, wide, keys, values = block_specs(length)
    stat_shape = jax.ShapeDtypeStruct((KVH, GROUP, length), F32)
    wide_shape = jax.ShapeDtypeStruct((Q_WIDTH, length), F32)
    low_shape = jax.ShapeDtypeStruct((Q_WIDTH, length), BF16)
    state = pl.pallas_call(
        forward_first,
        grid=(KVH,),
        in_specs=[wide, keys, values],
        out_specs=[stat, stat, wide],
        out_shape=[stat_shape, stat_shape, wide_shape],
        cost_estimate=costs(length, 2, 8),
        name="forward_first",
    )(queries, blocks[0], blocks[0])
    for step in range(1, len(blocks)):
        last = step == len(blocks) - 1
        state = pl.pallas_call(
            forward_last if last else forward_more,
            grid_spec=pltpu.PrefetchScalarGridSpec(
                num_scalar_prefetch=1,
                grid=(KVH,),
                in_specs=[wide, keys, values, stat, stat, wide],
                out_specs=[stat, wide, wide] if last else [stat, stat, wide],
                scratch_shapes=[pltpu.VMEM((1, GROUP, length), F32)] * 2 if last else [],
            ),
            out_shape=[stat_shape, wide_shape, low_shape]
            if last
            else [stat_shape, stat_shape, wide_shape],
            input_output_aliases={6: 1} if last else {4: 0, 5: 1, 6: 2},
            cost_estimate=costs(length, 2, 12),
            name="forward_last" if last else "forward_more",
        )(flags[step], queries, blocks[step], blocks[step], *state)
    return state


def backward_head(head, masked, q_ref, k_ref, v_ref, grad_ref, log_ref, delta):
    rows = pl.ds(head * HD, HD)
    query = q_ref[rows, :]
    grad = grad_ref[rows, :]
    scores = dot(k_ref[...], query, 0, 0)
    probs = jnp.exp2(scores * LOG2_SCALE - log_ref[0, head : head + 1, :])
    if masked:
        probs = jnp.where(visible(scores.shape[0]), probs, 0.0)
    grad_probs = dot(v_ref[...], grad, 0, 0)
    grad_scores = (probs * (grad_probs - delta)).astype(BF16)
    grad_query = dot(k_ref[...], grad_scores, 1, 0)
    grad_key = dot(query, grad_scores, 1, 1)
    grad_value = dot(grad, probs.astype(BF16), 1, 1)
    return grad_query, grad_key, grad_value


def backward_first(
    flag, q_ref, k_ref, v_ref, grad_ref, log_ref, attn_ref, delta_ref, dq_ref, dk_ref, dv_ref
):
    for head in range(GROUP):
        rows = pl.ds(head * HD, HD)
        delta_ref[0, head : head + 1, :] = jnp.sum(
            grad_ref[rows, :].astype(F32) * attn_ref[rows, :], axis=0, keepdims=True
        )

    @pl.when(flag[0] == 1)
    def _():
        for head in range(GROUP):
            rows = pl.ds(head * HD, HD)
            delta = delta_ref[0, head : head + 1, :]
            dq, dk, dv = backward_head(
                head, False, q_ref, k_ref, v_ref, grad_ref, log_ref, delta
            )
            dq_ref[rows, :] = dq
            dk_ref[...] = dk * SCALE if head == 0 else dk_ref[...] + dk * SCALE
            dv_ref[...] = dv if head == 0 else dv_ref[...] + dv

    @pl.when(flag[0] != 1)
    def _():
        dq_ref[...] = jnp.zeros_like(dq_ref)
        dk_ref[...] = jnp.zeros_like(dk_ref)
        dv_ref[...] = jnp.zeros_like(dv_ref)


def backward_more(
    masked, flag, q_ref, k_ref, v_ref, grad_ref, log_ref, delta_ref, dq_in, dq_ref, dk_ref, dv_ref
):
    @pl.when(flag[0] == 1)
    def _():
        for head in range(GROUP):
            rows = pl.ds(head * HD, HD)
            delta = delta_ref[0, head : head + 1, :]
            dq, dk, dv = backward_head(
                head, masked, q_ref, k_ref, v_ref, grad_ref, log_ref, delta
            )
            dq_ref[rows, :] = dq_in[rows, :] + dq
            dk_ref[...] = dk * SCALE if head == 0 else dk_ref[...] + dk * SCALE
            dv_ref[...] = dv if head == 0 else dv_ref[...] + dv

    @pl.when(flag[0] != 1)
    def _():
        dq_ref[...] = dq_in[...]
        dk_ref[...] = jnp.zeros_like(dk_ref)
        dv_ref[...] = jnp.zeros_like(dv_ref)


def attend_backward(queries, blocks, flags, grads, logs, attn, shift_down):
    length = queries.shape[1]
    count = len(blocks)
    stat, wide, keys, values = block_specs(length)
    stat_shape = jax.ShapeDtypeStruct((KVH, GROUP, length), F32)
    wide_shape = jax.ShapeDtypeStruct((Q_WIDTH, length), F32)
    key_shape = jax.ShapeDtypeStruct((KV_WIDTH, length), F32)
    arrived = None
    for step in range(count):
        back = count - 1 - step
        common = (flags[back], queries, blocks[back], blocks[back], grads, logs)
        if step == 0:
            delta, dq, dk, dv = pl.pallas_call(
                backward_first,
                grid_spec=pltpu.PrefetchScalarGridSpec(
                    num_scalar_prefetch=1,
                    grid=(KVH,),
                    in_specs=[wide, keys, values, wide, stat, wide],
                    out_specs=[stat, wide, keys, keys],
                ),
                out_shape=[stat_shape, wide_shape, key_shape, key_shape],
                cost_estimate=costs(length, 5, 20),
                name="backward_first",
            )(*common, attn)
        else:
            dq, dk, dv = pl.pallas_call(
                functools.partial(backward_more, back == 0),
                grid_spec=pltpu.PrefetchScalarGridSpec(
                    num_scalar_prefetch=1,
                    grid=(KVH,),
                    in_specs=[wide, keys, values, wide, stat, stat, wide],
                    out_specs=[wide, keys, keys],
                ),
                out_shape=[wide_shape, key_shape, key_shape],
                input_output_aliases={7: 0},
                cost_estimate=costs(length, 5, 20),
                name="backward_more",
            )(*common, delta, dq)
        fresh = jnp.concatenate([dk, dv], axis=0)
        if arrived is not None:
            fresh = fresh + arrived.astype(F32)
        if back > 0:
            arrived = shift_down(fresh.astype(BF16))
    return dq, fresh


def rotate(values, cosines, sines):
    parts = values.reshape(-1, 2, HALF, values.shape[1])
    first = parts[:, 0]
    second = parts[:, 1]
    return jnp.stack(
        [first * cosines - second * sines, second * cosines + first * sines], axis=1
    ).reshape(values.shape)


def norm_back(inputs, inverse, gain, grad_normed):
    scaled = grad_normed * gain
    inner = jnp.mean(scaled * inputs, axis=-1, keepdims=True)
    grad_inputs = inverse * scaled - inputs * inverse * inverse * inverse * inner
    grad_gain = jnp.sum(grad_normed * inputs * inverse, axis=0)
    return (grad_inputs, grad_gain)


def sum_over_ctx(share):
    count = lax.axis_size("ctx")
    place = lax.axis_index("ctx")
    bits = []
    distance = 1
    value = share
    while distance < count:
        rows = value.shape[0] // 2
        bit = (place // distance) % 2
        perm = [(i, i ^ distance) for i in range(count)]
        away = lax.dynamic_slice_in_dim(value, (1 - bit) * rows, rows, 0)
        keep = lax.dynamic_slice_in_dim(value, bit * rows, rows, 0)
        got = lax.ppermute(away, "ctx", perm)
        value = (keep.astype(F32) + got.astype(F32)).astype(BF16)
        bits.append((bit, perm))
        distance *= 2
    for bit, perm in reversed(bits):
        got = lax.ppermute(value, "ctx", perm)
        low = jnp.where(bit == 0, value, got)
        high = jnp.where(bit == 0, got, value)
        value = jnp.concatenate([low, high], axis=0)
    return value.astype(F32)


def local(layer_input, attn_gain, w_qkv, w_out, mlp_gain, w_gate_up, w_down, cotangent):
    length = layer_input.shape[1]
    count = lax.axis_size("ctx")
    place = lax.axis_index("ctx")
    up = [(i, i + 1) for i in range(count - 1)]
    down = [(i + 1, i) for i in range(count - 1)]

    def gather(shard):
        return lax.all_gather(shard, "dp", axis=0, tiled=True)

    def scatter(grad):
        return lax.psum_scatter(grad.astype(BF16), "dp", scatter_dimension=0, tiled=True)

    whole_kv = gather(w_qkv[:, Q_WIDTH:])
    whole_q = gather(w_qkv[:, :Q_WIDTH])
    whole_out = gather(w_out)
    whole_gu = gather(w_gate_up)
    whole_down = gather(w_down)
    gain_a = gather(attn_gain).astype(F32)
    gain_m = gather(mlp_gain).astype(F32)

    q_pos = place * length + jnp.arange(length, dtype=jnp.int32)
    freq = BASE ** (-(jnp.arange(HALF, dtype=F32) * 2.0 / HD))
    angle = freq[:, None] * q_pos.astype(F32)[None, :]
    cosines = jnp.cos(angle)
    sines = jnp.sin(angle)

    inputs = layer_input[0].astype(F32)
    inverse_a = lax.rsqrt(jnp.mean(inputs * inputs, axis=-1, keepdims=True) + EPS)
    normed_a = (inputs * inverse_a * gain_a).astype(BF16)

    proj_kv = dot(whole_kv, normed_a, 0, 1)
    k_rot = rotate(proj_kv[:KV_WIDTH], cosines, sines).astype(BF16)
    key_value = jnp.concatenate([k_rot, proj_kv[KV_WIDTH:].astype(BF16)], axis=0)
    blocks = [key_value]
    for _ in range(count - 1):
        blocks.append(lax.ppermute(blocks[-1], "ctx", up))
    flags = [(place >= step).astype(jnp.int32).reshape(1) for step in range(count)]
    q_rot = rotate(dot(whole_q, normed_a, 0, 1), cosines, sines).astype(BF16)

    logs, attn, attn_low = attend_forward(q_rot, blocks, flags)
    resid = inputs + dot(attn_low, whole_out, 0, 0)

    inverse_m = lax.rsqrt(jnp.mean(resid * resid, axis=-1, keepdims=True) + EPS)
    normed_m = (resid * inverse_m * gain_m).astype(BF16)
    gate_up = dot(normed_m, whole_gu, 1, 0)
    gate = gate_up[:, :FF]
    upper = gate_up[:, FF:]
    sigmoid = jax.nn.sigmoid(gate)
    act = (gate * sigmoid * upper).astype(BF16)
    grad_out = cotangent[0].astype(F32)
    grad_mlp = cotangent[0]
    down_share = scatter(dot(act, grad_mlp, 0, 0))
    result = (resid + dot(act, whole_down, 1, 0)).astype(BF16)
    grad_act = dot(grad_mlp, whole_down, 1, 1)
    grad_gate = grad_act * upper * sigmoid * (1.0 + gate * (1.0 - sigmoid))
    grad_up = grad_act * gate * sigmoid
    grad_gu = jnp.concatenate([grad_gate, grad_up], axis=1).astype(BF16)
    gu_share = scatter(dot(normed_m, grad_gu, 0, 0))
    grad_nm = dot(grad_gu, whole_gu, 1, 1)
    grad_res_m, gain_m_grad = norm_back(resid, inverse_m, gain_m, grad_nm)
    grad_resid = grad_out + grad_res_m
    grad_branch = grad_resid.astype(BF16)
    out_share = scatter(dot(attn_low, grad_branch, 1, 0))
    grad_attn = dot(whole_out, grad_branch, 1, 1).astype(BF16)

    grad_query, grad_kv = attend_backward(
        q_rot, blocks, flags, grad_attn, logs, attn, lambda x: lax.ppermute(x, "ctx", down)
    )
    gproj_q = rotate(grad_query * SCALE, cosines, -sines).astype(BF16)
    q_share = scatter(dot(normed_a, gproj_q, 0, 1))
    gproj_kv = jnp.concatenate(
        [rotate(grad_kv[:KV_WIDTH], cosines, -sines), grad_kv[KV_WIDTH:]], axis=0
    ).astype(BF16)
    kv_share = scatter(dot(normed_a, gproj_kv, 0, 1))
    grad_na = dot(gproj_q, whole_q, 0, 1) + dot(gproj_kv, whole_kv, 0, 1)
    grad_res_a, gain_a_grad = norm_back(inputs, inverse_a, gain_a, grad_na)
    input_grad = grad_resid + grad_res_a

    gains = lax.psum(jnp.stack([gain_a_grad, gain_m_grad]), ("dp", "ctx"))
    rows = attn_gain.shape[0]
    gains = lax.dynamic_slice_in_dim(gains, lax.axis_index("dp") * rows, rows, 1)
    return (
        result[None],
        input_grad[None],
        gains[0],
        jnp.concatenate([sum_over_ctx(q_share), sum_over_ctx(kv_share)], axis=1),
        sum_over_ctx(out_share),
        gains[1],
        sum_over_ctx(gu_share),
        sum_over_ctx(down_share),
    )


def solution(mesh):
    return jax.shard_map(
        local,
        mesh=mesh,
        in_specs=(
            P("dp", "ctx", None),
            P("dp"),
            P("dp", None),
            P("dp", None),
            P("dp"),
            P("dp", None),
            P("dp", None),
            P("dp", "ctx", None),
        ),
        out_specs=(
            P("dp", "ctx", None),
            P("dp", "ctx", None),
            P("dp"),
            P("dp", None),
            P("dp", None),
            P("dp"),
            P("dp", None),
            P("dp", None),
        ),
        check_vma=False,
    )
```
